512 devices in a mesh: chord: 64 (over z, x), span: 8 (over y, core).
Axes of the slice: x: 4, y: 4, z: 16, core: 2. Of those that a mesh axis runs over, the one named last changes fastest.
Arguments:
- adjoint_init: bfloat16 [64, 8, 3, 625, 128], P('chord', 'span'), may hold values from -6 to 6
- adjoint_rhs: bfloat16 [64, 8, 3, 625, 128], P('chord', 'span'), may hold values from -6 to 6
- block_inverse: bfloat16 [64, 8, 3, 625, 625], P('chord', 'span'), as said below
- flux_jacobian: float32 [64, 8, 3, 6, 5, 5, 25], P('chord', 'span'), may hold values from -2.5 to 2.5
- trace_ops: bfloat16 [4, 6, 25, 125], replicated, may hold values from -0.5 to 0.5
- shape_jacobian: bfloat16 [64, 8, 3, 81, 625], P('chord', 'span'), may hold values from -0.25 to 0.25
- element_order: int32 [64, 8, 3], P('chord', 'span'), may hold values from 1 to 4, as said below
- face_adjacency: int32 [64, 8, 3, 6], P('chord', 'span'), may hold values from -1 to 2, as said below
- node_owner: int32 [64, 8, 3, 27], P('chord', 'span'), may hold values from 0 to 159, as said below
Outputs:
- smoothed_adjoint: bfloat16 [64, 8, 3, 625, 128], P('chord', 'span')
- node_sensitivity: float32 [64, 8, 32, 3, 128], P('chord', 'span')
The draws below stay inside these ranges and needn't reach their ends.
Inputs may be any that keep to these rules, and one draw needn't show every extreme that they name: `element_order`: live unknowns of an element are its first 5 * min(125, (order + 1)**3). `face_adjacency`: entry [e, f] names the element beside face f in the partition that f faces (faces 0 and 1 previous and next along chord, cyclic; 2 and 3 previous and next along span; 4 and 5 the same partition), which meets it with its face f xor 1; -1 marks a boundary face (span ends, wall, far field). `node_owner`: entry k * 32 + i: owned node i of partition k, k = 0 the element's own, 1 and 2 previous and next along chord, 3 and 4 previous and next along span; k is never 3 on the first span partition nor 4 on the last. `block_inverse`: only the rows and columns of live unknowns act.
All inputs are finite; a program needn't handle non-finite values.
Results may differ from the reference program's by a relative error of at most 0.0069.
Values may be sent and summed in bfloat16 or wider, within the bound.
No kernel may reach another device: no remote copies, remote signals or barrier semaphores. Data moves between devices by JAX's collectives and lax.ppermute only.
A program may use at most 64 MiB of HBM per device.

```python
import math
import jax
import jax.numpy as jnp
from jax import lax

NODES = 125
VARS = 5
BLOCK = 625
FACEPTS = 25
GEO = 27
ELEMS = 3
OWNED = 32
RHS = 128
N_CHORD = 64
N_SPAN = 8


def column_order(key):
    scores = jax.random.randint(jax.random.fold_in(key, 11), (N_CHORD, N_SPAN, ELEMS), 0, 1 << 20)
    scores = scores * ELEMS + jnp.arange(ELEMS, dtype=jnp.int32)
    placed = jnp.argsort(scores, axis=-1).astype(jnp.int32)
    position = jnp.argsort(placed, axis=-1).astype(jnp.int32)
    return (placed, position)


def draw_element_order(key, part):
    placed, position = column_order(key)
    levels = 4 - 3 * position // ELEMS
    drops = jax.random.randint(jax.random.fold_in(key, 12), (N_CHORD, N_SPAN, ELEMS), 0, 2)
    chord_ids = jnp.arange(N_CHORD, dtype=jnp.int32)[:, None, None]
    leading = (chord_ids < max(1, N_CHORD // 8)).astype(jnp.int32)
    orders = jnp.clip(levels - drops + leading, 1, 4).astype(jnp.int32)
    return orders.at[N_CHORD - 1, N_SPAN - 1, 0].set(1)


def draw_face_adjacency(key, part):
    placed, position = column_order(key)
    no_span = -jnp.ones((N_CHORD, 1, ELEMS), jnp.int32)
    no_level = -jnp.ones((N_CHORD, N_SPAN, 1), jnp.int32)
    prev_chord = jnp.roll(placed, 1, axis=0)
    next_chord = jnp.roll(placed, -1, axis=0)
    prev_span = jnp.concatenate([no_span, placed[:, :-1]], axis=1)
    next_span = jnp.concatenate([placed[:, 1:], no_span], axis=1)
    below = jnp.concatenate([no_level, placed[:, :, :-1]], axis=2)
    above = jnp.concatenate([placed[:, :, 1:], no_level], axis=2)
    face_lists = [jnp.take_along_axis(source, position, axis=2) for source in (prev_chord, next_chord, prev_span, next_span, below, above)]
    return jnp.stack(face_lists, axis=-1).astype(jnp.int32)


def draw_node_owner(key, part):
    codes = jax.random.randint(jax.random.fold_in(key, 21), (N_CHORD, N_SPAN, ELEMS, GEO), 0, 5)
    span_ids = jnp.arange(N_SPAN, dtype=jnp.int32)[None, :, None, None]
    codes = jnp.where((span_ids == 0) & (codes == 3), 0, codes)
    codes = jnp.where((span_ids == N_SPAN - 1) & (codes == 4), 0, codes)
    slots = jax.random.randint(jax.random.fold_in(key, 22), (N_CHORD, N_SPAN, ELEMS, GEO), 0, OWNED)
    owners = (codes * OWNED + slots).astype(jnp.int32)
    owners = owners.at[0, 0, 0, 0].set(0)
    return owners.at[0, 0, 0, 1].set(5 * OWNED - 1)


def draw_block_inverse(key, part):
    shape = (N_CHORD, N_SPAN, ELEMS, BLOCK, BLOCK)
    key_diag = jax.random.fold_in(key, 31)
    key_off = jax.random.fold_in(key, 32)
    diagonal_mask = jnp.arange(BLOCK)[:, None] == jnp.arange(BLOCK)[None, :]
    diag_vals = jnp.exp(jax.random.uniform(key_diag, shape[:-1] + (1,), jnp.float32, math.log(0.5), math.log(2.0)))
    spread = jax.random.normal(key_off, shape, jnp.float32) * (0.6 / math.sqrt(BLOCK))
    blocks = jnp.where(diagonal_mask, diag_vals, 0.0) + spread
    return blocks.astype(jnp.bfloat16)


def block_scale(stream_key, dims, cuts, least, high):
    gain, own = 1.0, jax.random.fold_in(stream_key, 6)
    for dim, blocks in cuts:
        steps = jnp.exp(jax.random.uniform(jax.random.fold_in(own, dim), (blocks,), jnp.float32, least / len(cuts), high / len(cuts)))
        gain = gain * jnp.repeat(steps, dims[dim] // blocks).reshape([-1 if axis == dim else 1 for axis in range(len(dims))])
    return gain


def gaussian(own_key, extent, deviation, reach, cuts=(), held_as=jnp.bfloat16):
    loudness = block_scale(own_key, extent, cuts, -0.22, 0.18) if cuts else 1.0
    array = jax.random.normal(own_key, extent, jnp.float32) * deviation * loudness
    return jnp.minimum(jnp.maximum(array, -reach), reach).astype(held_as)


def setup_inputs(seed: int = 0) -> dict:
    key_list = jax.random.split(jax.random.key(seed), 10)
    adjoint_init = gaussian(key_list[0], (N_CHORD, N_SPAN, ELEMS, BLOCK, RHS), 1.0, 6.0, ((0, 64), (1, 8)))
    adjoint_rhs = gaussian(key_list[1], (N_CHORD, N_SPAN, ELEMS, BLOCK, RHS), 1.0, 6.0, ((0, 64), (1, 8)))
    block_inverse = draw_block_inverse(jax.random.fold_in(key_list[9], 71), 0)
    flux_jacobian = gaussian(key_list[3], (N_CHORD, N_SPAN, ELEMS, 6, VARS, VARS, FACEPTS), VARS ** -0.5, 2.5, ((0, 64), (1, 8)), jnp.float32)
    trace_ops = gaussian(key_list[4], (4, 6, FACEPTS, NODES), NODES ** -0.5, 0.5)
    shape_jacobian = gaussian(key_list[5], (N_CHORD, N_SPAN, ELEMS, GEO * 3, BLOCK), BLOCK ** -0.5, 0.25, ((0, 64), (1, 8)))
    element_order = draw_element_order(jax.random.fold_in(key_list[9], 71), 0)
    face_adjacency = draw_face_adjacency(jax.random.fold_in(key_list[9], 71), 0)
    node_owner = draw_node_owner(jax.random.fold_in(key_list[9], 71), 0)
    return {"adjoint_init": adjoint_init, "adjoint_rhs": adjoint_rhs, "block_inverse": block_inverse, "flux_jacobian": flux_jacobian, "trace_ops": trace_ops, "shape_jacobian": shape_jacobian, "element_order": element_order, "face_adjacency": face_adjacency, "node_owner": node_owner}


HIGH = lax.Precision.HIGHEST


def active_rows(element_order):
    live_count = jnp.minimum((element_order + 1) ** 3, NODES) * VARS
    return (jnp.arange(BLOCK, dtype=jnp.int32) < live_count[..., None]).astype(jnp.float32)


def incoming(trace_tiles, face_adjacency):
    zero_row = jnp.zeros_like(trace_tiles[:, :1, :, 0])
    sources = [jnp.roll(trace_tiles[:, :, :, 1], 1, axis=0),
               jnp.roll(trace_tiles[:, :, :, 0], -1, axis=0),
               jnp.concatenate([zero_row, trace_tiles[:, :-1, :, 3]], axis=1),
               jnp.concatenate([trace_tiles[:, 1:, :, 2], zero_row], axis=1),
               trace_tiles[:, :, :, 5],
               trace_tiles[:, :, :, 4]]
    pieces = []
    for face_id in range(6):
        neighbour = face_adjacency[:, :, :, face_id]
        safe_ids = jnp.maximum(neighbour, 0).astype(jnp.int32)
        picked = jnp.take_along_axis(sources[face_id], safe_ids[:, :, :, None, None, None], axis=2)
        pieces.append(jnp.where(neighbour[:, :, :, None, None, None] >= 0, picked, jnp.zeros_like(picked)))
    return jnp.stack(pieces, axis=3)


def reference(adjoint_init, adjoint_rhs, block_inverse, flux_jacobian, trace_ops, shape_jacobian, element_order, face_adjacency, node_owner):
    row_mask = active_rows(element_order)
    trace_wide = trace_ops.astype(jnp.float32)

    def tiles_of_row(operands):
        adjoint, poly_orders, flux_blocks = operands
        table = jnp.take(trace_wide, poly_orders - 1, axis=0)
        volume = adjoint.astype(jnp.float32).reshape(N_SPAN, ELEMS, NODES, VARS, RHS)
        trace_vals = jnp.einsum('sefqk,sekvr->sefqvr', table, volume, precision=HIGH)
        tiles = jnp.einsum('sefwvq,sefqwr->sefqvr', flux_blocks, trace_vals, precision=HIGH)
        return tiles.astype(jnp.bfloat16)

    def update_row(operands):
        inflow, poly_orders, rhs_row, inverse_row, mask_row = operands
        table = jnp.take(trace_wide, poly_orders - 1, axis=0)
        coupling = jnp.einsum('sefqk,sefqvr->sekvr', table, inflow.astype(jnp.float32), precision=HIGH)
        coupling = coupling.reshape(N_SPAN, ELEMS, BLOCK, RHS)
        driven = (mask_row[..., None] * (rhs_row.astype(jnp.float32) - coupling)).astype(jnp.bfloat16)
        solved = jnp.einsum('seij,sejr->seir', inverse_row.astype(jnp.float32), driven.astype(jnp.float32), precision=HIGH)
        return (solved * mask_row[..., None]).astype(jnp.bfloat16)

    adjoint = (adjoint_init.astype(jnp.float32) * row_mask[..., None]).astype(jnp.bfloat16)
    for sweep_id in range(2):
        trace_tiles = lax.map(tiles_of_row, (adjoint, element_order, flux_jacobian))
        inflow = incoming(trace_tiles, face_adjacency)
        adjoint = lax.map(update_row, (inflow, element_order, adjoint_rhs, block_inverse, row_mask))

    def sense_row(operands):
        jac_row, adjoint_row, owner_row = operands
        partials = jnp.einsum('segb,sebr->segr', jac_row.astype(jnp.float32), adjoint_row.astype(jnp.float32), precision=HIGH)
        flat_parts = partials.reshape(N_SPAN, ELEMS * GEO, 3 * RHS)
        slot_ids = jnp.arange(5 * OWNED, dtype=jnp.int32)
        onehot = (slot_ids[None, :, None] == owner_row.reshape(N_SPAN, 1, ELEMS * GEO)).astype(jnp.float32)
        summed = jnp.einsum('skj,sjm->skm', onehot, flat_parts, precision=HIGH)
        return summed.reshape(N_SPAN, 5, OWNED, 3, RHS)

    buffers = lax.map(sense_row, (shape_jacobian, adjoint, node_owner))
    zero_row = jnp.zeros_like(buffers[:, :1, 0])
    result = buffers[:, :, 0]
    result = result + jnp.roll(buffers[:, :, 1], -1, axis=0)
    result = result + jnp.roll(buffers[:, :, 2], 1, axis=0)
    result = result + jnp.concatenate([buffers[:, 1:, 3], zero_row], axis=1)
    result = result + jnp.concatenate([zero_row, buffers[:, :-1, 4]], axis=1)
    return adjoint, result
```

```python
import jax
import jax.numpy as jnp
from jax import lax
from jax.experimental import pallas as pl
from jax.experimental.pallas import tpu as pltpu
from jax.sharding import PartitionSpec as P


ELEMS = 3
NODES = 125
VARS = 5
BLOCK = 625
PTS = 25
GEO = 27
OWNED = 32
RHS = 128
FROWS = 128
SENS = 3 * OWNED
PITCH = 32

ISSUE_ORDER = ("B", "A", "D", "C")
SLOT_AXIS = {"A": "chord", "B": "chord", "C": "span", "D": "span"}
F32 = jnp.float32
BF16 = jnp.bfloat16


def swap_pairs(slot, size):
    cyclic = SLOT_AXIS[slot] == "chord"
    first = 0 if slot in "AC" else 1
    last = size if cyclic else size - 1
    pairs = []
    for i in range(first, last, 2):
        j = (i + 1) % size
        pairs += [(i, j), (j, i)]
    return pairs


def exchange(sends):
    received = []
    for i, slot in enumerate(ISSUE_ORDER):
        axis = SLOT_AXIS[slot]
        received.append(lax.ppermute(sends[i], axis, swap_pairs(slot, lax.axis_size(axis))))
    return received


def slot_faces():
    chord_odd = lax.axis_index("chord") % 2
    span_odd = lax.axis_index("span") % 2
    faces = {"A": 1 - chord_odd, "B": chord_odd, "C": 3 - span_odd, "D": 2 + span_odd}
    return [faces[slot] for slot in ISSUE_ORDER]


def dot(a, b, dims=((1,), (0,))):
    return lax.dot_general(a, b, (dims, ((), ())), preferred_element_type=F32)


def iota(shape, dim):
    return lax.broadcasted_iota(jnp.int32, shape, dim)


def one_of(value, choices):
    hit = value == choices[0]
    for choice in choices[1:]:
        hit = hit | (value == choice)
    return hit


def point_spread(order):
    gap = 4 * iota((FROWS, PTS * 4), 0) + order - 1 - iota((FROWS, PTS * 4), 1)
    return one_of(gap, [v * PTS * 4 for v in range(VARS)]).astype(BF16)


def node_spread(shape, node_dim):
    gap = iota(shape, 1 - node_dim) - VARS * iota(shape, node_dim)
    return ((gap >= 0) & (gap < VARS)).astype(BF16)


def live_mask(order, shape):
    count = VARS * jnp.minimum((order + 1) * (order + 1) * (order + 1), NODES)
    return iota(shape, 0) < count


def variable_of(unknown):
    node = ((unknown.astype(F32) + 0.5) * (1.0 / VARS)).astype(jnp.int32)
    return unknown - VARS * node


def build_trace_rows(rows_ref, order_ref, faces, trace_ref):
    count = len(faces)
    spreads = [point_spread(order_ref[0, 0, e]) for e in range(ELEMS)]
    for s, face in enumerate(faces):
        levels = trace_ref[face].astype(F32).reshape(PTS * 4, NODES).astype(BF16)
        for e in range(ELEMS):
            at = (e * count + s) * FROWS
            rows_ref[at : at + FROWS, :] = dot(spreads[e], levels).astype(BF16)


def build_face_operator(op_ref, faces, flux_ref, rows_ref, line_ref):
    count = len(faces)
    line_ref[...] = jnp.zeros(line_ref.shape, F32)
    for e in range(ELEMS):
        for s, face in enumerate(faces):
            for w in range(VARS):
                first = ((e * 6 + face) * VARS + w) * VARS
                line_ref[e * count + s, w, 0:VARS, 0:PTS] = flux_ref[pl.ds(first, VARS), 0, :]
    columns = []
    for w in range(VARS):
        lines = []
        for i in range(ELEMS * count):
            moved = pltpu.roll(line_ref[i, w], 0, 1, stride=PTS // 2, stride_axis=0)
            moved = pltpu.roll(moved, 0, 1, stride=PTS - PTS // 2, stride_axis=0)
            lines.append(jnp.sum(moved, axis=0, keepdims=True))
        columns.append(jnp.concatenate(lines, axis=1))
    flux_lines = jnp.concatenate(columns, axis=0)
    high = flux_lines.astype(BF16)
    low = (flux_lines - high.astype(F32)).astype(BF16)
    pair = jnp.concatenate([high.astype(F32), low.astype(F32)], axis=0)
    line = iota((2 * VARS, BLOCK), 0)
    picks = (variable_of(iota((2 * VARS, BLOCK), 1)) == variable_of(line)).astype(BF16)
    factors = dot(pair.T.astype(BF16), picks)
    nodes = node_spread((NODES, BLOCK), 0)
    wide = dot(rows_ref[...], nodes)
    op = (wide * factors).astype(BF16)
    for e in range(ELEMS):
        op_ref[e] = op[e * count * FROWS : (e + 1) * count * FROWS]


def build_trace_points(points_ref, order_ref, faces, trace_ref):
    for s, face in enumerate(faces):
        levels = trace_ref[face].astype(F32).reshape(PTS * 4, NODES).astype(BF16)
        for e in range(ELEMS):
            shape = (PITCH, PTS * 4)
            pick = 4 * iota(shape, 0) + order_ref[0, 0, e] - 1 == iota(shape, 1)
            rows = dot(pick.astype(F32).astype(BF16), levels).astype(BF16)
            points_ref[e, s * PITCH : (s + 1) * PITCH, :] = rows


def coupling(points, inflows, wide_ref, out_ref):
    for s, inflow in enumerate(inflows):
        rows = inflow.astype(F32)
        for v in range(VARS):
            at = slice(s * PITCH, s * PITCH + PTS)
            wide_ref[at, v * RHS : (v + 1) * RHS] = rows[v * PTS : (v + 1) * PTS]
    sums = dot(points, wide_ref[...].astype(BF16), ((0,), (0,)))
    for v in range(VARS):
        out_ref[pl.ds(v, NODES, stride=VARS), :] = sums[:, v * RHS : (v + 1) * RHS]
    return out_ref[...]


def start_copies(pairs, sems):
    copies = [pltpu.make_async_copy(src, dst, sems.at[i]) for i, (src, dst) in enumerate(pairs)]
    for copy in copies:
        copy.start()
    return copies


def first_tiles_kernel(order_hbm, adjoint_hbm, flux_hbm, trace_hbm, *refs):
    sends, (op_ref, adjoint_ref, flux_ref, trace_ref) = refs[:4], refs[4:8]
    rows_ref, line_ref, order_ref, sems = refs[8:]
    sources = (order_hbm, trace_hbm, flux_hbm, adjoint_hbm)
    copies = start_copies(zip(sources, (order_ref, trace_ref, flux_ref, adjoint_ref)), sems)
    faces = slot_faces()
    copies[0].wait()
    copies[1].wait()
    build_trace_rows(rows_ref, order_ref, faces, trace_ref)
    copies[2].wait()
    build_face_operator(op_ref, faces, flux_ref, rows_ref, line_ref)
    copies[3].wait()
    for e in range(ELEMS):
        live = live_mask(order_ref[0, 0, e], (BLOCK, RHS))
        adjoint = jnp.where(live, adjoint_ref[0, 0, e], jnp.zeros((), BF16))
        tiles = dot(op_ref[e], adjoint).astype(BF16)
        for s in range(4):
            sends[s][e] = tiles[s * FROWS : (s + 1) * FROWS]


def local_driven(near_ref, adjoints, rhs_ref, op_ref, points_ref, tile_ref, wide_ref, sum_ref, out_ref):
    wide_ref[...] = jnp.zeros(wide_ref.shape, F32)
    for e in range(ELEMS):
        tile_ref[e] = dot(op_ref[e], adjoints(e)).astype(BF16)
    for e in range(ELEMS):
        pieces = []
        for face in (4, 5):
            near = near_ref[e, 0, face]
            at = (5 - face) * FROWS
            picked = tile_ref[jnp.maximum(near, 0), at : at + FROWS, :]
            pieces.append(jnp.where(near >= 0, picked, jnp.zeros((), BF16)))
        total = coupling(points_ref[e], pieces, wide_ref.at[e], sum_ref.at[e])
        out_ref[e] = rhs_ref[0, 0, e].astype(F32) - total


def prepare_kernel(order_hbm, near_hbm, rhs_hbm, inverse_hbm, adjoint_ref, flux_ref, trace_ref, *refs):
    base_ref, points_ref, local_op_ref, local_points_ref, rhs_ref, inverse_ref = refs[:6]
    rows_ref, line_ref, tile_ref, wide_ref, sum_ref, order_ref, near_ref, sems = refs[6:]
    sources = (order_hbm, near_hbm, rhs_hbm, inverse_hbm)
    copies = start_copies(zip(sources, (order_ref, near_ref, rhs_ref, inverse_ref)), sems)
    copies[0].wait()
    build_trace_rows(rows_ref, order_ref, [4, 5], trace_ref)
    build_face_operator(local_op_ref, [4, 5], flux_ref, rows_ref, line_ref)
    build_trace_points(local_points_ref, order_ref, [4, 5], trace_ref)
    build_trace_points(points_ref, order_ref, slot_faces(), trace_ref)

    def adjoints(e):
        live = live_mask(order_ref[0, 0, e], (BLOCK, RHS))
        return jnp.where(live, adjoint_ref[0, 0, e], jnp.zeros((), BF16))

    copies[1].wait()
    copies[2].wait()
    local_driven(
        near_ref, adjoints, rhs_ref, local_op_ref, local_points_ref,
        tile_ref, wide_ref, sum_ref, base_ref,
    )
    copies[3].wait()


def local_kernel(
    order_ref, near_ref, adjoint_ref, rhs_ref, local_op_ref, local_points_ref,
    base_ref, tile_ref, wide_ref, sum_ref,
):
    local_driven(
        near_ref, lambda e: adjoint_ref[e], rhs_ref, local_op_ref, local_points_ref,
        tile_ref, wide_ref, sum_ref, base_ref,
    )


def solve_blocks(
    faces, order_ref, near_ref, base_ref, arrived, points_ref, inverse_ref, wide_ref, sum_ref
):
    wide_ref[...] = jnp.zeros(wide_ref.shape, F32)
    driven = []
    for e in range(ELEMS):
        pieces = []
        for s, face in enumerate(faces):
            near = near_ref[e, 0, face]
            picked = arrived[s][jnp.maximum(near, 0)]
            pieces.append(jnp.where(near >= 0, picked, jnp.zeros((), BF16)))
        total = coupling(points_ref[e], pieces, wide_ref.at[e], sum_ref.at[e])
        live = live_mask(order_ref[0, 0, e], (BLOCK, RHS))
        driven.append(jnp.where(live, base_ref[e] - total, 0.0).astype(BF16))
    solved = []
    for e in range(ELEMS):
        live = live_mask(order_ref[0, 0, e], (BLOCK, RHS))
        solved.append(jnp.where(live, dot(inverse_ref[0, 0, e], driven[e]), 0.0).astype(BF16))
    return solved


def sweep_kernel(order_ref, near_ref, base_ref, a0, a1, a2, a3, points_ref, inverse_ref, op_ref, *refs):
    sends, (adjoint_ref, wide_ref, sum_ref) = refs[:4], refs[4:]
    solved = solve_blocks(
        slot_faces(), order_ref, near_ref, base_ref, (a0, a1, a2, a3), points_ref, inverse_ref,
        wide_ref, sum_ref,
    )
    for e in range(ELEMS):
        adjoint_ref[e] = solved[e]
        tiles = dot(op_ref[e], solved[e]).astype(BF16)
        for s in range(4):
            sends[s][e] = tiles[s * FROWS : (s + 1) * FROWS]


def last_kernel(
    order_ref, near_ref, base_ref, a0, a1, a2, a3, points_ref, inverse_ref, shape_ref, owner_ref, *refs
):
    adjoint_ref, own_ref, sends, (wide_ref, sum_ref) = refs[0], refs[1], refs[2:6], refs[6:]
    faces = slot_faces()
    owner = owner_ref[:, 0, :].astype(F32).astype(BF16)
    gap = iota((GEO, 3 * GEO), 1) - 3 * iota((GEO, 3 * GEO), 0)
    owners = dot(owner, ((gap >= 0) & (gap < 3)).astype(BF16))
    row = iota((SENS, 3 * GEO), 0)
    coordinate = (row >= OWNED).astype(jnp.int32) + (row >= 2 * OWNED).astype(jnp.int32)
    slot = (row - OWNED * coordinate).astype(F32)
    column = iota((SENS, 3 * GEO), 1)
    fits = column - 3 * ((column.astype(F32) + 0.5) * (1.0 / 3)).astype(jnp.int32) == coordinate
    solved = solve_blocks(
        faces, order_ref, near_ref, base_ref, (a0, a1, a2, a3), points_ref, inverse_ref,
        wide_ref, sum_ref,
    )
    total = jnp.zeros((5 * SENS, RHS), F32)
    for e in range(ELEMS):
        adjoint_ref[0, 0, e] = solved[e]
        partial = dot(shape_ref[0, 0, e], solved[e])
        high = partial.astype(BF16)
        low = (partial - high.astype(F32)).astype(BF16)
        picks = []
        for first in [0] + [OWNED * (face + 1) for face in faces]:
            hit = owners[e : e + 1, :] - jnp.asarray(first, jnp.int32).astype(F32) == slot
            picks.append((hit & fits).astype(F32).astype(BF16))
        picks = jnp.concatenate(picks, axis=0)
        total = total + dot(picks, high) + dot(picks, low)
    own_ref[...] = total[:SENS]
    for s in range(4):
        sends[s][...] = total[(s + 1) * SENS : (s + 2) * SENS].astype(BF16)


def sum_kernel(own_ref, a0, a1, a2, a3, out_ref):
    total = own_ref[...]
    for arrived in (a0, a1, a2, a3):
        total = total + arrived[...].astype(F32)
    for c in range(3):
        out_ref[0, 0, c] = total[c * OWNED : (c + 1) * OWNED]


SMEM = pl.BlockSpec(memory_space=pltpu.SMEM)
VMEM = pl.BlockSpec(memory_space=pltpu.VMEM)
ANY = pl.BlockSpec(memory_space=pl.ANY)
LIMIT = 24 * 1024 * 1024


def call(kernel, scalars, stored, held, outs, scratch=()):
    stored = [pltpu.with_memory_space_constraint(x, pltpu.HBM) for x in stored]
    held = [pltpu.with_memory_space_constraint(x, pltpu.VMEM) for x in held]
    return pl.pallas_call(
        kernel,
        in_specs=[SMEM] * len(scalars) + [ANY] * len(stored) + [VMEM] * len(held),
        out_specs=[VMEM] * len(outs),
        out_shape=outs,
        scratch_shapes=list(scratch),
        compiler_params=pltpu.CompilerParams(vmem_limit_bytes=LIMIT),
    )(*scalars, *stored, *held)


def body(
    adjoint_init,
    adjoint_rhs,
    block_inverse,
    flux_jacobian,
    trace_ops,
    shape_jacobian,
    element_order,
    face_adjacency,
    node_owner,
):
    held = pltpu.VMEM
    near = face_adjacency.reshape(ELEMS, 1, 6)
    owner = node_owner.reshape(ELEMS, 1, GEO)
    flux = flux_jacobian.reshape(ELEMS * 6 * VARS * VARS, 1, PTS)
    trace = jnp.transpose(trace_ops, (1, 2, 0, 3))
    face_send = [held((ELEMS, FROWS, RHS), BF16)] * 4
    base_shape = held((ELEMS, BLOCK, RHS), F32)
    near_sums = [pltpu.VMEM((ELEMS, 2 * PITCH, VARS * RHS), F32), pltpu.VMEM((ELEMS, BLOCK, RHS), F32)]
    far_sums = [pltpu.VMEM((ELEMS, 4 * PITCH, VARS * RHS), F32), pltpu.VMEM((ELEMS, BLOCK, RHS), F32)]
    order_smem = pltpu.SMEM(element_order.shape, jnp.int32)
    near_smem = pltpu.SMEM(near.shape, jnp.int32)
    *sends, face_op, adjoint, flux, trace = call(
        first_tiles_kernel,
        [],
        [element_order, adjoint_init, flux, trace],
        [],
        face_send
        + [
            held((ELEMS, 4 * FROWS, BLOCK), BF16),
            held(adjoint_init.shape, BF16),
            held(flux.shape, F32),
            held(trace.shape, BF16),
        ],
        [
            pltpu.VMEM((ELEMS * 4 * FROWS, NODES), BF16),
            pltpu.VMEM((ELEMS * 4, VARS, 8, 128), F32),
            order_smem,
            pltpu.SemaphoreType.DMA((4,)),
        ],
    )
    arrived = exchange(sends)
    base, points, local_op, local_points, rhs, inverse = call(
        prepare_kernel,
        [],
        [element_order, near, adjoint_rhs, block_inverse],
        [adjoint, flux, trace],
        [
            base_shape,
            held((ELEMS, 4 * PITCH, NODES), BF16),
            held((ELEMS, 2 * FROWS, BLOCK), BF16),
            held((ELEMS, 2 * PITCH, NODES), BF16),
            held(adjoint_rhs.shape, BF16),
            held(block_inverse.shape, BF16),
        ],
        [
            pltpu.VMEM((ELEMS * 2 * FROWS, NODES), BF16),
            pltpu.VMEM((ELEMS * 2, VARS, 8, 128), F32),
            pltpu.VMEM((ELEMS, 2 * FROWS, RHS), BF16),
            *near_sums,
            order_smem,
            near_smem,
            pltpu.SemaphoreType.DMA((4,)),
        ],
    )
    *sends, adjoint = call(
        sweep_kernel,
        [element_order, near],
        [],
        [base, *arrived, points, inverse, face_op],
        face_send + [held((ELEMS, BLOCK, RHS), BF16)],
        far_sums,
    )
    arrived = exchange(sends)
    (base,) = call(
        local_kernel,
        [element_order, near],
        [],
        [adjoint, rhs, local_op, local_points],
        [base_shape],
        [pltpu.VMEM((ELEMS, 2 * FROWS, RHS), BF16), *near_sums],
    )
    smoothed, own, *sends = call(
        last_kernel,
        [element_order, near],
        [],
        [base, *arrived, points, inverse, shape_jacobian, owner],
        [held((1, 1, ELEMS, BLOCK, RHS), BF16), held((SENS, RHS), F32)]
        + [held((SENS, RHS), BF16)] * 4,
        far_sums,
    )
    arrived = exchange(sends)
    (summed,) = call(
        sum_kernel, [], [], [own, *arrived], [jax.ShapeDtypeStruct((1, 1, 3, OWNED, RHS), F32)]
    )
    return smoothed, jnp.transpose(summed, (0, 1, 3, 2, 4))


def solution(mesh):
    placed = (
        P("chord", "span", None, None, None),
        P("chord", "span", None, None, None),
        P("chord", "span", None, None, None),
        P("chord", "span", None, None, None, None, None),
        P(),
        P("chord", "span", None, None, None),
        P("chord", "span", None),
        P("chord", "span", None, None),
        P("chord", "span", None, None),
    )
    return jax.shard_map(
        body,
        mesh=mesh,
        in_specs=placed,
        out_specs=(P("chord", "span", None, None, None), P("chord", "span", None, None, None)),
        check_vma=False,
    )
```

```python
import jax
import jax.numpy as jnp
from jax import lax
from jax.experimental import pallas as pl
from jax.experimental.pallas import tpu as pltpu
from jax.sharding import PartitionSpec as P


ELEMS = 3
NODES = 125
VARS = 5
BLOCK = 625
PTS = 25
GEO = 27
OWNED = 32
RHS = 128
FROWS = 128
SENS = 3 * OWNED
PITCH = 32

ISSUE_ORDER = ("B", "A", "D", "C")
SLOT_AXIS = {"A": "chord", "B": "chord", "C": "span", "D": "span"}
F32 = jnp.float32
BF16 = jnp.bfloat16


def swap_pairs(slot, size):
    cyclic = SLOT_AXIS[slot] == "chord"
    first = 0 if slot in "AC" else 1
    last = size if cyclic else size - 1
    pairs = []
    for i in range(first, last, 2):
        j = (i + 1) % size
        pairs += [(i, j), (j, i)]
    return pairs


def exchange(sends):
    received = []
    for i, slot in enumerate(ISSUE_ORDER):
        axis = SLOT_AXIS[slot]
        received.append(lax.ppermute(sends[i], axis, swap_pairs(slot, lax.axis_size(axis))))
    return received


def slot_faces():
    chord_odd = lax.axis_index("chord") % 2
    span_odd = lax.axis_index("span") % 2
    faces = {"A": 1 - chord_odd, "B": chord_odd, "C": 3 - span_odd, "D": 2 + span_odd}
    return [faces[slot] for slot in ISSUE_ORDER]


def dot(a, b, dims=((1,), (0,))):
    return lax.dot_general(a, b, (dims, ((), ())), preferred_element_type=F32)


def iota(shape, dim):
    return lax.broadcasted_iota(jnp.int32, shape, dim)


def one_of(value, choices):
    hit = value == choices[0]
    for choice in choices[1:]:
        hit = hit | (value == choice)
    return hit


def point_spread(order):
    gap = 4 * iota((FROWS, PTS * 4), 0) + order - 1 - iota((FROWS, PTS * 4), 1)
    return one_of(gap, [v * PTS * 4 for v in range(VARS)]).astype(BF16)


def node_spread(shape, node_dim):
    gap = iota(shape, 1 - node_dim) - VARS * iota(shape, node_dim)
    return ((gap >= 0) & (gap < VARS)).astype(BF16)


def live_mask(order, shape):
    count = VARS * jnp.minimum((order + 1) * (order + 1) * (order + 1), NODES)
    return iota(shape, 0) < count


def variable_of(unknown):
    node = ((unknown.astype(F32) + 0.5) * (1.0 / VARS)).astype(jnp.int32)
    return unknown - VARS * node


def build_trace_rows(rows_ref, order_ref, faces, trace_ref):
    count = len(faces)
    spreads = [point_spread(order_ref[0, 0, e]) for e in range(ELEMS)]
    for s, face in enumerate(faces):
        levels = trace_ref[face].astype(F32).reshape(PTS * 4, NODES).astype(BF16)
        for e in range(ELEMS):
            at = (e * count + s) * FROWS
            rows_ref[at : at + FROWS, :] = dot(spreads[e], levels).astype(BF16)


def flux_factors(faces, flux_ref, line_ref):
    count = len(faces)
    line_ref[...] = jnp.zeros(line_ref.shape, F32)
    for e in range(ELEMS):
        for s, face in enumerate(faces):
            for w in range(VARS):
                first = ((e * 6 + face) * VARS + w) * VARS
                line_ref[e * count + s, w, 0:VARS, 0:PTS] = flux_ref[pl.ds(first, VARS), 0, :]
    columns = []
    for w in range(VARS):
        lines = []
        for i in range(ELEMS * count):
            moved = pltpu.roll(line_ref[i, w], 0, 1, stride=PTS // 2, stride_axis=0)
            moved = pltpu.roll(moved, 0, 1, stride=PTS - PTS // 2, stride_axis=0)
            lines.append(jnp.sum(moved, axis=0, keepdims=True))
        columns.append(jnp.concatenate(lines, axis=1))
    flux_lines = jnp.concatenate(columns, axis=0)
    high = flux_lines.astype(BF16)
    low = (flux_lines - high.astype(F32)).astype(BF16)
    pair = jnp.concatenate([high.astype(F32), low.astype(F32)], axis=0)
    line = iota((2 * VARS, BLOCK), 0)
    picks = (variable_of(iota((2 * VARS, BLOCK), 1)) == variable_of(line)).astype(BF16)
    return pair.T.astype(BF16), picks


def build_face_operator(op_ref, e, count, factors, rows_ref):
    at = slice(e * count * FROWS, (e + 1) * count * FROWS)
    wide = dot(rows_ref[at, :], node_spread((NODES, BLOCK), 0))
    op_ref[e] = (wide * dot(factors[0][at], factors[1])).astype(BF16)


def build_trace_points(points_ref, order_ref, faces, trace_ref):
    for s, face in enumerate(faces):
        levels = trace_ref[face].astype(F32).reshape(PTS * 4, NODES).astype(BF16)
        for e in range(ELEMS):
            shape = (PITCH, PTS * 4)
            pick = 4 * iota(shape, 0) + order_ref[0, 0, e] - 1 == iota(shape, 1)
            rows = dot(pick.astype(F32).astype(BF16), levels).astype(BF16)
            points_ref[e, s * PITCH : (s + 1) * PITCH, :] = rows


def coupling(points, inflows, wide_ref, out_ref):
    for s, inflow in enumerate(inflows):
        rows = inflow.astype(F32)
        for v in range(VARS):
            at = slice(s * PITCH, s * PITCH + PTS)
            wide_ref[at, v * RHS : (v + 1) * RHS] = rows[v * PTS : (v + 1) * PTS]
    sums = dot(points, wide_ref[...].astype(BF16), ((0,), (0,)))
    for v in range(VARS):
        out_ref[pl.ds(v, NODES, stride=VARS), :] = sums[:, v * RHS : (v + 1) * RHS]
    return out_ref[...]


def start_copies(pairs, sems):
    copies = [pltpu.make_async_copy(src, dst, sems.at[i]) for i, (src, dst) in enumerate(pairs)]
    for copy in copies:
        copy.start()
    return copies


def first_tiles_kernel(order_hbm, adjoint_hbm, flux_hbm, trace_hbm, *refs):
    sends, (op_ref, adjoint_ref, flux_ref, trace_ref) = refs[:4], refs[4:8]
    rows_ref, line_ref, order_ref, sems = refs[8:]
    sources = (order_hbm, trace_hbm, flux_hbm, adjoint_hbm)
    copies = start_copies(zip(sources, (order_ref, trace_ref, flux_ref, adjoint_ref)), sems)
    faces = slot_faces()
    for copy in copies:
        copy.wait()
    build_trace_rows(rows_ref, order_ref, faces, trace_ref)
    factors = flux_factors(faces, flux_ref, line_ref)
    for e in range(ELEMS):
        build_face_operator(op_ref, e, 4, factors, rows_ref)
        live = live_mask(order_ref[0, 0, e], (BLOCK, RHS))
        adjoint = jnp.where(live, adjoint_ref[0, 0, e], jnp.zeros((), BF16))
        tiles = dot(op_ref[e], adjoint).astype(BF16)
        for s in range(4):
            sends[s][e] = tiles[s * FROWS : (s + 1) * FROWS]


def local_driven(near_ref, adjoints, rhs_ref, op_ref, points_ref, tile_ref, wide_ref, sum_ref, out_ref):
    wide_ref[...] = jnp.zeros(wide_ref.shape, F32)
    for e in range(ELEMS):
        tile_ref[e] = dot(op_ref[e], adjoints(e)).astype(BF16)
    for e in range(ELEMS):
        pieces = []
        for face in (4, 5):
            near = near_ref[e, 0, face]
            at = (5 - face) * FROWS
            picked = tile_ref[jnp.maximum(near, 0), at : at + FROWS, :]
            pieces.append(jnp.where(near >= 0, picked, jnp.zeros((), BF16)))
        total = coupling(points_ref[e], pieces, wide_ref.at[e], sum_ref.at[e])
        out_ref[e] = rhs_ref[0, 0, e].astype(F32) - total


def prepare_kernel(order_hbm, near_hbm, rhs_hbm, inverse_hbm, adjoint_ref, flux_ref, trace_ref, *refs):
    base_ref, points_ref, local_op_ref, local_points_ref, rhs_ref, inverse_ref = refs[:6]
    rows_ref, line_ref, tile_ref, wide_ref, sum_ref, order_ref, near_ref, sems = refs[6:]
    sources = (order_hbm, near_hbm, rhs_hbm, inverse_hbm)
    copies = start_copies(zip(sources, (order_ref, near_ref, rhs_ref, inverse_ref)), sems)
    factors = flux_factors([4, 5], flux_ref, line_ref)
    for copy in copies[:3]:
        copy.wait()
    build_trace_rows(rows_ref, order_ref, [4, 5], trace_ref)
    for e in range(ELEMS):
        build_face_operator(local_op_ref, e, 2, factors, rows_ref)
    build_trace_points(local_points_ref, order_ref, [4, 5], trace_ref)
    build_trace_points(points_ref, order_ref, slot_faces(), trace_ref)

    def adjoints(e):
        live = live_mask(order_ref[0, 0, e], (BLOCK, RHS))
        return jnp.where(live, adjoint_ref[0, 0, e], jnp.zeros((), BF16))

    local_driven(
        near_ref, adjoints, rhs_ref, local_op_ref, local_points_ref,
        tile_ref, wide_ref, sum_ref, base_ref,
    )
    copies[3].wait()


def local_kernel(
    order_ref, near_ref, adjoint_ref, rhs_ref, local_op_ref, local_points_ref,
    base_ref, tile_ref, wide_ref, sum_ref,
):
    local_driven(
        near_ref, lambda e: adjoint_ref[e], rhs_ref, local_op_ref, local_points_ref,
        tile_ref, wide_ref, sum_ref, base_ref,
    )


def solve_blocks(
    faces, order_ref, near_ref, base_ref, arrived, points_ref, inverse_ref, wide_ref, sum_ref
):
    wide_ref[...] = jnp.zeros(wide_ref.shape, F32)
    driven = []
    for e in range(ELEMS):
        pieces = []
        for s, face in enumerate(faces):
            near = near_ref[e, 0, face]
            picked = arrived[s][jnp.maximum(near, 0)]
            pieces.append(jnp.where(near >= 0, picked, jnp.zeros((), BF16)))
        total = coupling(points_ref[e], pieces, wide_ref.at[e], sum_ref.at[e])
        live = live_mask(order_ref[0, 0, e], (BLOCK, RHS))
        driven.append(jnp.where(live, base_ref[e] - total, 0.0).astype(BF16))
    solved = []
    for e in range(ELEMS):
        live = live_mask(order_ref[0, 0, e], (BLOCK, RHS))
        solved.append(jnp.where(live, dot(inverse_ref[0, 0, e], driven[e]), 0.0).astype(BF16))
    return solved


def sweep_kernel(order_ref, near_ref, base_ref, a0, a1, a2, a3, points_ref, inverse_ref, op_ref, *refs):
    sends, (adjoint_ref, wide_ref, sum_ref) = refs[:4], refs[4:]
    solved = solve_blocks(
        slot_faces(), order_ref, near_ref, base_ref, (a0, a1, a2, a3), points_ref, inverse_ref,
        wide_ref, sum_ref,
    )
    for e in range(ELEMS):
        adjoint_ref[e] = solved[e]
        tiles = dot(op_ref[e], solved[e]).astype(BF16)
        for s in range(4):
            sends[s][e] = tiles[s * FROWS : (s + 1) * FROWS]


def last_kernel(
    order_ref, near_ref, base_ref, a0, a1, a2, a3, points_ref, inverse_ref, shape_ref, owner_ref, *refs
):
    adjoint_ref, own_ref, sends, (wide_ref, sum_ref) = refs[0], refs[1], refs[2:6], refs[6:]
    faces = slot_faces()
    owner = owner_ref[:, 0, :].astype(F32).astype(BF16)
    gap = iota((GEO, 3 * GEO), 1) - 3 * iota((GEO, 3 * GEO), 0)
    owners = dot(owner, ((gap >= 0) & (gap < 3)).astype(BF16))
    row = iota((SENS, 3 * GEO), 0)
    coordinate = (row >= OWNED).astype(jnp.int32) + (row >= 2 * OWNED).astype(jnp.int32)
    slot = (row - OWNED * coordinate).astype(F32)
    column = iota((SENS, 3 * GEO), 1)
    fits = column - 3 * ((column.astype(F32) + 0.5) * (1.0 / 3)).astype(jnp.int32) == coordinate
    solved = solve_blocks(
        faces, order_ref, near_ref, base_ref, (a0, a1, a2, a3), points_ref, inverse_ref,
        wide_ref, sum_ref,
    )
    total = jnp.zeros((5 * SENS, RHS), F32)
    for e in range(ELEMS):
        adjoint_ref[0, 0, e] = solved[e]
        partial = dot(shape_ref[0, 0, e], solved[e])
        high = partial.astype(BF16)
        low = (partial - high.astype(F32)).astype(BF16)
        picks = []
        for first in [0] + [OWNED * (face + 1) for face in faces]:
            hit = owners[e : e + 1, :] - jnp.asarray(first, jnp.int32).astype(F32) == slot
            picks.append((hit & fits).astype(F32).astype(BF16))
        picks = jnp.concatenate(picks, axis=0)
        total = total + dot(picks, high) + dot(picks, low)
    own_ref[...] = total[:SENS]
    for s in range(4):
        sends[s][...] = total[(s + 1) * SENS : (s + 2) * SENS].astype(BF16)


def sum_kernel(own_ref, a0, a1, a2, a3, out_ref):
    total = own_ref[...]
    for arrived in (a0, a1, a2, a3):
        total = total + arrived[...].astype(F32)
    for c in range(3):
        out_ref[0, 0, c] = total[c * OWNED : (c + 1) * OWNED]


SMEM = pl.BlockSpec(memory_space=pltpu.SMEM)
VMEM = pl.BlockSpec(memory_space=pltpu.VMEM)
ANY = pl.BlockSpec(memory_space=pl.ANY)
LIMIT = 24 * 1024 * 1024


def call(kernel, scalars, stored, held, outs, scratch=()):
    stored = [pltpu.with_memory_space_constraint(x, pltpu.HBM) for x in stored]
    held = [pltpu.with_memory_space_constraint(x, pltpu.VMEM) for x in held]
    return pl.pallas_call(
        kernel,
        in_specs=[SMEM] * len(scalars) + [ANY] * len(stored) + [VMEM] * len(held),
        out_specs=[VMEM] * len(outs),
        out_shape=outs,
        scratch_shapes=list(scratch),
        compiler_params=pltpu.CompilerParams(vmem_limit_bytes=LIMIT),
    )(*scalars, *stored, *held)


def body(
    adjoint_init,
    adjoint_rhs,
    block_inverse,
    flux_jacobian,
    trace_ops,
    shape_jacobian,
    element_order,
    face_adjacency,
    node_owner,
):
    held = pltpu.VMEM
    near = face_adjacency.reshape(ELEMS, 1, 6)
    owner = node_owner.reshape(ELEMS, 1, GEO)
    flux = flux_jacobian.reshape(ELEMS * 6 * VARS * VARS, 1, PTS)
    trace = jnp.transpose(trace_ops, (1, 2, 0, 3))
    face_send = [held((ELEMS, FROWS, RHS), BF16)] * 4
    base_shape = held((ELEMS, BLOCK, RHS), F32)
    near_sums = [pltpu.VMEM((ELEMS, 2 * PITCH, VARS * RHS), F32), pltpu.VMEM((ELEMS, BLOCK, RHS), F32)]
    far_sums = [pltpu.VMEM((ELEMS, 4 * PITCH, VARS * RHS), F32), pltpu.VMEM((ELEMS, BLOCK, RHS), F32)]
    order_smem = pltpu.SMEM(element_order.shape, jnp.int32)
    near_smem = pltpu.SMEM(near.shape, jnp.int32)
    *sends, face_op, adjoint, flux, trace = call(
        first_tiles_kernel,
        [],
        [element_order, adjoint_init, flux, trace],
        [],
        face_send
        + [
            held((ELEMS, 4 * FROWS, BLOCK), BF16),
            held(adjoint_init.shape, BF16),
            held(flux.shape, F32),
            held(trace.shape, BF16),
        ],
        [
            pltpu.VMEM((ELEMS * 4 * FROWS, NODES), BF16),
            pltpu.VMEM((ELEMS * 4, VARS, 8, 128), F32),
            order_smem,
            pltpu.SemaphoreType.DMA((4,)),
        ],
    )
    arrived = exchange(sends)
    base, points, local_op, local_points, rhs, inverse = call(
        prepare_kernel,
        [],
        [element_order, near, adjoint_rhs, block_inverse],
        [adjoint, flux, trace],
        [
            base_shape,
            held((ELEMS, 4 * PITCH, NODES), BF16),
            held((ELEMS, 2 * FROWS, BLOCK), BF16),
            held((ELEMS, 2 * PITCH, NODES), BF16),
            held(adjoint_rhs.shape, BF16),
            held(block_inverse.shape, BF16),
        ],
        [
            pltpu.VMEM((ELEMS * 2 * FROWS, NODES), BF16),
            pltpu.VMEM((ELEMS * 2, VARS, 8, 128), F32),
            pltpu.VMEM((ELEMS, 2 * FROWS, RHS), BF16),
            *near_sums,
            order_smem,
            near_smem,
            pltpu.SemaphoreType.DMA((4,)),
        ],
    )
    *sends, adjoint = call(
        sweep_kernel,
        [element_order, near],
        [],
        [base, *arrived, points, inverse, face_op],
        face_send + [held((ELEMS, BLOCK, RHS), BF16)],
        far_sums,
    )
    arrived = exchange(sends)
    (base,) = call(
        local_kernel,
        [element_order, near],
        [],
        [adjoint, rhs, local_op, local_points],
        [base_shape],
        [pltpu.VMEM((ELEMS, 2 * FROWS, RHS), BF16), *near_sums],
    )
    smoothed, own, *sends = call(
        last_kernel,
        [element_order, near],
        [],
        [base, *arrived, points, inverse, shape_jacobian, owner],
        [held((1, 1, ELEMS, BLOCK, RHS), BF16), held((SENS, RHS), F32)]
        + [held((SENS, RHS), BF16)] * 4,
        far_sums,
    )
    arrived = exchange(sends)
    (summed,) = call(
        sum_kernel, [], [], [own, *arrived], [jax.ShapeDtypeStruct((1, 1, 3, OWNED, RHS), F32)]
    )
    return smoothed, jnp.transpose(summed, (0, 1, 3, 2, 4))


def solution(mesh):
    placed = (
        P("chord", "span", None, None, None),
        P("chord", "span", None, None, None),
        P("chord", "span", None, None, None),
        P("chord", "span", None, None, None, None, None),
        P(),
        P("chord", "span", None, None, None),
        P("chord", "span", None),
        P("chord", "span", None, None),
        P("chord", "span", None, None),
    )
    return jax.shard_map(
        body,
        mesh=mesh,
        in_specs=placed,
        out_specs=(P("chord", "span", None, None, None), P("chord", "span", None, None, None)),
        check_vma=False,
    )
```
